256 devices in a mesh: sec: 32 (over x_hi, z, core), mpo: 8 (over y, x_lo).
Axes of the slice: x: 4 (x_hi: 2, x_lo: 2; x = x_hi * 2 + x_lo), y: 4, z: 8, core: 2. Of those that a mesh axis runs over, the one named last changes fastest.
Arguments:
- two_site: bfloat16 [512, 128, 128], P('sec'), may hold values from -6 to 6
- left_env: bfloat16 [64, 64, 128, 128], P('mpo', 'sec'), may hold values from -0.5 to 0.5
- right_env: bfloat16 [64, 64, 128, 128], P('mpo', 'sec'), may hold values from -0.5 to 0.5
- left_sector: int32 [512], P('sec'), may hold values from 0 to 63, as said below
- right_sector: int32 [512], P('sec'), may hold values from 0 to 63, as said below
- mpo_weight: float32 [64, 4], P('mpo'), may hold values from -0.75 to 0.75
- src_slot: int32 [512, 4], P('sec'), may hold values from 0 to 15
- joining: float32 [512, 4], P('sec'), may hold values from -4 to 4
Outputs:
- applied_state: bfloat16 [512, 128, 128], P('sec', 'mpo')
The draws below stay inside these ranges and needn't reach their ends.
Inputs may be any that keep to these rules, and one draw needn't show every extreme that they name: `left_sector`: block k's left sector is one held by the same index of sec as the block: between 2 * (k // 16) and that plus 2 - 1. `right_sector`: block k's right sector is one held by the same index of sec as the block: between 2 * (k // 16) and that plus 2 - 1.
All inputs are finite; a program needn't handle non-finite values.
Results may differ from the reference program's by a relative error of at most 0.0049.
Values sent between devices are 32-bit elements; how exact they have to be, the bound alone decides.
No kernel may reach another device: no remote copies, remote signals or barrier semaphores. Data moves between devices by JAX's collectives and lax.ppermute only.
A program may use at most 64 MiB of HBM per device.

```python
import jax
import jax.numpy as jnp
from jax import lax

BLK = 128
WB = 64
CHAN = 4
NS_DEV = 2
NB_DEV = 16
NS = 64
NB = 512
N_SEC = 32


def sector_draw(key, salt):
    local = jax.random.randint(jax.random.fold_in(key, salt), (NB,), 0, NS_DEV)
    owner = jnp.arange(NB, dtype=jnp.int32) // NB_DEV
    return (owner * NS_DEV + local).astype(jnp.int32)


def draw_left_sector(key, part):
    return sector_draw(key, 11)


def draw_right_sector(key, part):
    return sector_draw(key, 23)


def touch_ends(entries, rng, least, high):
    dims = entries.shape
    place = [jax.random.randint(jax.random.fold_in(rng, axis), (), 0, dims[axis]) for axis in range(len(dims))]
    entries = entries.at[tuple(place)].set(least)
    longest = dims.index(max(dims))
    place[longest] = (place[longest] + 1) % dims[longest]
    return entries.at[tuple(place)].set(high)


def level_of(stream_key, dims, pieces, least, largest):
    def one(dim, shards_of):
        draws = jax.random.uniform(jax.random.fold_in(jax.random.fold_in(stream_key, 6), dim), (shards_of,), jnp.float32, least / len(pieces), largest / len(pieces))
        return jnp.repeat(jnp.exp(draws), dims[dim] // shards_of).reshape((-1,) + (1,) * (len(dims) - dim - 1))

    factor_of = one(*pieces[0])
    for cut in pieces[1:]:
        factor_of = factor_of * one(*cut)
    return factor_of


def normal_values(key, dims, spread, reach, shards=(), kind=jnp.bfloat16):
    values = jax.random.normal(key, dims, jnp.float32) * spread
    if len(shards) > 0:
        values = level_of(key, dims, shards, -0.22, 0.18) * values
    return jnp.clip(values, min=-reach, max=reach).astype(kind)


def setup_inputs(seed: int = 0) -> dict:
    streams_of = jax.random.split(jax.random.key(seed), 9)
    two_site = normal_values(streams_of[0], (NB, BLK, BLK), 1.0, 6.0, ((0, 32),))
    left_env = normal_values(streams_of[1], (WB, NS, BLK, BLK), BLK ** -0.5, 0.5, ((0, 8), (1, 32)))
    right_env = normal_values(streams_of[2], (WB, NS, BLK, BLK), BLK ** -0.5, 0.5, ((0, 8), (1, 32)))
    left_sector = draw_left_sector(jax.random.fold_in(streams_of[8], 71), 0)
    right_sector = draw_right_sector(jax.random.fold_in(streams_of[8], 71), 0)
    mpo_weight = normal_values(streams_of[5], (WB, CHAN), WB ** -0.5, 0.75, ((0, 8),), jnp.float32)
    src_slot = touch_ends(jax.random.randint(streams_of[6], (NB, CHAN), 0, NB_DEV), jax.random.fold_in(streams_of[6], 1), 0, NB_DEV - 1).astype(jnp.int32)
    joining = normal_values(streams_of[7], (NB, CHAN), 0.5, 4.0, ((0, 32),), jnp.float32)
    return {"two_site": two_site, "left_env": left_env, "right_env": right_env, "left_sector": left_sector, "right_sector": right_sector, "mpo_weight": mpo_weight, "src_slot": src_slot, "joining": joining}


def reference(two_site, left_env, right_env, left_sector, right_sector, mpo_weight, src_slot, joining):
    group = 8
    count = NB // group

    def one_group(items):
        blocks, left_ids, right_ids = items
        left_blocks = jnp.take(left_env, left_ids, axis=1).astype(jnp.float32)
        right_blocks = jnp.take(right_env, right_ids, axis=1).astype(jnp.float32)
        product = jnp.einsum("wgac,gcd->wgad", left_blocks, blocks.astype(jnp.float32)).astype(jnp.bfloat16)
        applied = jnp.einsum("wgad,wgbd->wgab", product.astype(jnp.float32), right_blocks)
        return jnp.einsum("wf,wgab->gfab", mpo_weight, applied, precision=lax.Precision.HIGHEST)

    grouped = (two_site.reshape(count, group, BLK, BLK), left_sector.reshape(count, group), right_sector.reshape(count, group))
    channel_sums = lax.map(one_group, grouped).reshape(NB, CHAN, BLK, BLK)
    owner = jnp.arange(NB, dtype=jnp.int32) // NB_DEV
    shifts = [0, -1, 1, -(N_SEC // 2)]
    summed = jnp.zeros((NB, BLK, BLK), jnp.float32)
    for channel in range(CHAN):
        source = ((owner + shifts[channel]) % N_SEC) * NB_DEV + src_slot[:, channel]
        picked = channel_sums[source.astype(jnp.int32), channel]
        summed = summed + joining[:, channel][:, None, None] * picked
    return summed.astype(jnp.bfloat16)
```

```python
import jax
import jax.numpy as jnp
from jax import lax
from jax.experimental import pallas as pl
from jax.experimental.pallas import tpu as pltpu
from jax.sharding import PartitionSpec as P


BLK = 128
W = 8
NB = 16
CH = 4
N_SEC = 32
N_MPO = 8
ROWS = BLK // N_MPO
DEEP = W * BLK
GROUP = 4
BOTH = ("sec", "mpo")
HOPS = ((2, 1), (1, 1), (2, 0), (1, 0), (3, 1), (0, 1), (3, 0))

SMEM = pl.BlockSpec(memory_space=pltpu.SMEM)
VMEM = pl.BlockSpec(memory_space=pltpu.VMEM)
F32 = jnp.float32
BF16 = jnp.bfloat16


def place(m, hop):
    return (((m // 2) + hop[0]) % 4) * 2 + ((m % 2) + hop[1]) % 2


def over_mpo(x, hop):
    return lax.ppermute(x, "mpo", [(m, place(m, hop)) for m in range(N_MPO)])


def over_both(x, target):
    pairs = []
    for s in range(N_SEC):
        for m in range(N_MPO):
            to_s, to_m = target(s, m)
            pairs.append((s * N_MPO + m, (to_s % N_SEC) * N_MPO + to_m))
    return lax.ppermute(x, BOTH, pairs)


def scale_right(right, weight, channel, scaled):
    for w in range(W):
        factor = weight[channel, w]
        for s in range(2):
            part = right[w, s].astype(F32) * factor
            scaled[s * BLK : (s + 1) * BLK, w * BLK : (w + 1) * BLK] = part.astype(BF16)


def one_channel(product, scaled, right_sector, store):
    for g in range(NB // GROUP):
        rows = product[g * GROUP : (g + 1) * GROUP].reshape(GROUP * BLK, DEEP)
        both = lax.dot_general(
            rows, scaled[...], (((1,), (1,)), ((), ())), preferred_element_type=F32
        )
        for i in range(GROUP):
            k = g * GROUP + i
            mine = both[i * BLK : (i + 1) * BLK]
            second = (right_sector[k] & 1) == 1
            store(k, jnp.where(second, mine[:, BLK:], mine[:, :BLK]))


def first_kernel(
    left_sector, right_sector, weight, two_site, left, right, product, lower, upper, wide, scaled
):
    for w in range(W):
        for s in range(2):
            wide[w * BLK : (w + 1) * BLK, s * BLK : (s + 1) * BLK] = left[w, s]
    for pair in range(NB // 2):
        columns = []
        for i in range(2):
            k = 2 * pair + i
            block = two_site[k]
            second = (left_sector[k] & 1) == 1
            zero = jnp.zeros_like(block)
            columns.append(
                jnp.concatenate(
                    [jnp.where(second, zero, block), jnp.where(second, block, zero)], axis=0
                )
            )
        out = jnp.dot(
            wide[...], jnp.concatenate(columns, axis=1), preferred_element_type=F32
        ).astype(BF16)
        for i in range(2):
            for w in range(W):
                product[2 * pair + i, :, w * BLK : (w + 1) * BLK] = out[
                    w * BLK : (w + 1) * BLK, i * BLK : (i + 1) * BLK
                ]
    for channel, ref in ((1, lower), (2, upper)):
        scale_right(right, weight, channel, scaled)

        def store(k, value, ref=ref):
            ref[k] = value

        one_channel(product, scaled, right_sector, store)


def opposite_kernel(right_sector, weight, right, product, *rest):
    outs, (scaled, whole) = rest[: N_MPO], rest[N_MPO:]
    scale_right(right, weight, 3, scaled)

    def store(k, value):
        whole[k] = value

    one_channel(product, scaled, right_sector, store)
    m = lax.axis_index("mpo")
    for out, hop in zip(outs, HOPS + ((0, 0),)):
        start = pl.multiple_of(place(m, hop) * ROWS, ROWS)
        out[...] = whole[:, pl.ds(start, ROWS), :]


def own_kernel(right_sector, weight, right, product, own, scaled):
    scale_right(right, weight, 0, scaled)

    def store(k, value):
        own[k] = value

    one_channel(product, scaled, right_sector, store)


def join_kernel(src_slot, joining, own, lower, upper, *outs):
    m = lax.axis_index("mpo")
    for k in range(NB):
        for out, hop in zip(outs, HOPS + ((0, 0),)):
            start = pl.multiple_of(place(m, hop) * ROWS, ROWS)
            part = joining[0, k] * own[src_slot[0, k], pl.ds(start, ROWS), :]
            part = part + joining[1, k] * lower[src_slot[1, k], pl.ds(start, ROWS), :]
            part = part + joining[2, k] * upper[src_slot[2, k], pl.ds(start, ROWS), :]
            out[k] = part


def last_kernel(src_slot, joining, opposite, *rest):
    parts, result = rest[:-1], rest[-1]
    for k in range(NB):
        total = joining[3, k] * opposite[src_slot[3, k]]
        for part in parts:
            total = total + part[k]
        result[k] = total.astype(BF16)


def params(mib):
    return pltpu.CompilerParams(vmem_limit_bytes=mib * 2**20)


def cost(flops, read):
    return pl.CostEstimate(flops=flops, bytes_accessed=read, transcendentals=0)


def per_device(
    two_site, left_env, right_env, left_sector, right_sector, mpo_weight, src_slot, joining
):
    mpo_weight, src_slot, joining = mpo_weight.T, src_slot.T, joining.T
    shape = jax.ShapeDtypeStruct
    sums = shape((NB, BLK, BLK), F32)
    slab = shape((NB, ROWS, BLK), F32)
    scaled = pltpu.VMEM((2 * BLK, DEEP), BF16)
    matmul = 2 * NB * BLK * DEEP * 2 * BLK
    product, to_lower, to_upper = pl.pallas_call(
        first_kernel,
        in_specs=[SMEM, SMEM, SMEM, VMEM, VMEM, VMEM],
        out_specs=[VMEM, VMEM, VMEM],
        out_shape=[shape((NB, BLK, DEEP), BF16), sums, sums],
        scratch_shapes=[pltpu.VMEM((DEEP, 2 * BLK), BF16), scaled],
        cost_estimate=cost(3 * matmul, 2**23),
        compiler_params=params(2),
        name="product_and_neighbours",
    )(left_sector, right_sector, mpo_weight, two_site, left_env, right_env)
    lower = over_both(to_lower, lambda s, m: (s + 1, m ^ 1 if s % 16 == 15 else m))
    upper = over_both(to_upper, lambda s, m: (s - 1, m ^ 1 if s % 16 == 0 else m))
    slabs = pl.pallas_call(
        opposite_kernel,
        in_specs=[SMEM, SMEM, VMEM, VMEM],
        out_specs=[VMEM] * N_MPO,
        out_shape=[slab] * N_MPO,
        scratch_shapes=[scaled, pltpu.VMEM((NB, BLK, BLK), F32)],
        cost_estimate=cost(matmul, 2**22),
        compiler_params=params(5),
        name="opposite_sums",
    )(right_sector, mpo_weight, right_env, product)
    opposite = slabs[-1]
    moved = [over_mpo(x, hop) for x, hop in zip(slabs, HOPS)]
    own = pl.pallas_call(
        own_kernel,
        in_specs=[SMEM, SMEM, VMEM, VMEM],
        out_specs=VMEM,
        out_shape=sums,
        scratch_shapes=[scaled],
        cost_estimate=cost(matmul, 2**22),
        compiler_params=params(5),
        name="own_sums",
    )(right_sector, mpo_weight, right_env, product)
    for part in moved:
        opposite = opposite + part
    opposite = over_both(opposite, lambda s, m: (s + N_SEC // 2, m))
    slabs = pl.pallas_call(
        join_kernel,
        in_specs=[SMEM, SMEM, VMEM, VMEM, VMEM],
        out_specs=[VMEM] * N_MPO,
        out_shape=[slab] * N_MPO,
        cost_estimate=cost(2**21, 2**22),
        compiler_params=params(2),
        name="join_blocks",
    )(src_slot, joining, own, lower, upper)
    moved = [over_mpo(x, hop) for x, hop in zip(slabs, HOPS)]
    return pl.pallas_call(
        last_kernel,
        in_specs=[SMEM, SMEM] + [VMEM] * (N_MPO + 1),
        out_specs=VMEM,
        out_shape=shape((NB, ROWS, BLK), BF16),
        cost_estimate=cost(2**18, 2**20),
        compiler_params=params(2),
        name="sum_and_round",
    )(src_slot, joining, opposite, *moved, slabs[-1])


def solution(mesh):
    placed = (
        P("sec", None, None),
        P("mpo", "sec", None, None),
        P("mpo", "sec", None, None),
        P("sec"),
        P("sec"),
        P("mpo", None),
        P("sec", None),
        P("sec", None),
    )
    return jax.shard_map(
        per_device, mesh=mesh, in_specs=placed, out_specs=P("sec", "mpo", None), check_vma=False
    )
```

```python
import jax
import jax.numpy as jnp
from jax import lax
from jax.experimental import pallas as pl
from jax.experimental.pallas import tpu as pltpu
from jax.sharding import PartitionSpec as P


BLK = 128
W = 8
NB = 16
CH = 4
N_SEC = 32
N_MPO = 8
ROWS = BLK // N_MPO
DEEP = W * BLK
BOTH = ("sec", "mpo")
HOPS = ((2, 1), (1, 1), (2, 0), (1, 0), (3, 1), (0, 1), (3, 0))

Y_HOPS = (2, 1, 3)

HBM = pl.BlockSpec(memory_space=pltpu.HBM)
SMEM = pl.BlockSpec(memory_space=pltpu.SMEM)
VMEM = pl.BlockSpec(memory_space=pltpu.VMEM)
F32 = jnp.float32
BF16 = jnp.bfloat16


def place(m, hop):
    return (((m // 2) + hop[0]) % 4) * 2 + ((m % 2) + hop[1]) % 2


def over_mpo(x, hop):
    return lax.ppermute(x, "mpo", [(m, place(m, hop)) for m in range(N_MPO)])


def over_both(x, target):
    pairs = []
    for s in range(N_SEC):
        for m in range(N_MPO):
            to_s, to_m = target(s, m)
            pairs.append((s * N_MPO + m, (to_s % N_SEC) * N_MPO + to_m))
    return lax.ppermute(x, BOTH, pairs)


def scale_right(right, weight, channels, scaled):
    for w in range(W):
        for s in range(2):
            block = right[w, s].astype(F32)
            for i, channel in enumerate(channels):
                part = (block * weight[channel, w]).astype(BF16)
                scaled[s, i * BLK : (i + 1) * BLK, w * BLK : (w + 1) * BLK] = part


def two_channels(product, scaled, right_sector, first, second):
    for k in range(NB):
        both = lax.dot_general(
            product[k],
            scaled[right_sector[k] & 1],
            (((1,), (1,)), ((), ())),
            preferred_element_type=F32,
        )
        first[k] = both[:, :BLK]
        second[k] = both[:, BLK:]


def first_kernel(
    left_sector_in,
    right_sector_in,
    weight_in,
    two_site_in,
    left_in,
    right_in,
    product,
    lower,
    upper,
    left_sector,
    right_sector,
    weight,
    two_site,
    wide,
    right,
    scaled,
    small_sems,
    big_sems,
    wide_sems,
):
    copies = [
        pltpu.make_async_copy(left_sector_in, left_sector, small_sems.at[0]),
        pltpu.make_async_copy(right_sector_in, right_sector, small_sems.at[1]),
        pltpu.make_async_copy(weight_in, weight, small_sems.at[2]),
        pltpu.make_async_copy(two_site_in, two_site, big_sems.at[0]),
    ]
    for s in range(2):
        copies.append(
            pltpu.make_async_copy(
                left_in.at[:, s], wide.at[:, :, s * BLK : (s + 1) * BLK], wide_sems.at[s]
            )
        )
    last = pltpu.make_async_copy(right_in, right, big_sems.at[1])
    for copy in copies:
        copy.start()
    last.start()
    for copy in copies:
        copy.wait()
    for pair in range(NB // 2):
        columns = []
        for i in range(2):
            k = 2 * pair + i
            block = two_site[k]
            second = (left_sector[k] & 1) == 1
            zero = jnp.zeros_like(block)
            columns.append(
                jnp.concatenate(
                    [jnp.where(second, zero, block), jnp.where(second, block, zero)], axis=0
                )
            )
        out = jnp.dot(
            wide[...].reshape(DEEP, 2 * BLK),
            jnp.concatenate(columns, axis=1),
            preferred_element_type=F32,
        ).astype(BF16)
        for i in range(2):
            for w in range(W):
                product[2 * pair + i, :, w * BLK : (w + 1) * BLK] = out[
                    w * BLK : (w + 1) * BLK, i * BLK : (i + 1) * BLK
                ]
    last.wait()
    scale_right(right, weight, (1, 2), scaled)
    two_channels(product, scaled, right_sector, lower, upper)


def second_kernel(right_sector, weight, right, product, own, *rest):
    outs, (scaled, whole) = rest[: len(Y_HOPS) + 1], rest[len(Y_HOPS) + 1 :]
    scale_right(right, weight, (3, 0), scaled)
    two_channels(product, scaled, right_sector, whole, own)
    m = lax.axis_index("mpo")
    for out, steps in zip(outs, Y_HOPS + (0,)):
        for flip in range(2):
            start = pl.multiple_of(place(m, (steps, flip)) * ROWS, ROWS)
            out[flip] = whole[:, pl.ds(start, ROWS), :]


def join_kernel(src_slot, joining, own, lower, upper, *outs):
    m = lax.axis_index("mpo")
    for k in range(NB):
        for out, hop in zip(outs, HOPS + ((0, 0),)):
            start = pl.multiple_of(place(m, hop) * ROWS, ROWS)
            part = joining[0, k] * own[src_slot[0, k], pl.ds(start, ROWS), :]
            part = part + joining[1, k] * lower[src_slot[1, k], pl.ds(start, ROWS), :]
            part = part + joining[2, k] * upper[src_slot[2, k], pl.ds(start, ROWS), :]
            out[k] = part


def last_kernel(src_slot, joining, straight, crossed, *rest):
    parts, result = rest[:-1], rest[-1]
    for k in range(NB):
        slot = src_slot[3, k]
        total = joining[3, k] * (straight[slot] + crossed[slot])
        for part in parts:
            total = total + part[k]
        result[k] = total.astype(BF16)


def in_hbm(x):
    return pltpu.with_memory_space_constraint(x, pltpu.HBM)


def params(mib):
    return pltpu.CompilerParams(vmem_limit_bytes=mib * 2**20)


def cost(flops, read):
    return pl.CostEstimate(flops=flops, bytes_accessed=read, transcendentals=0)


def per_device(
    two_site, left_env, right_env, left_sector, right_sector, mpo_weight, src_slot, joining
):
    mpo_weight, src_slot, joining = mpo_weight.T, src_slot.T, joining.T
    shape = jax.ShapeDtypeStruct
    sums = shape((NB, BLK, BLK), F32)
    slab = shape((NB, ROWS, BLK), F32)
    wide_slab = shape((2, NB, ROWS, BLK), F32)
    scaled = pltpu.VMEM((2, 2 * BLK, DEEP), BF16)
    matmul = 2 * NB * BLK * DEEP * 2 * BLK
    product, to_lower, to_upper = pl.pallas_call(
        first_kernel,
        in_specs=[HBM] * 6,
        out_specs=[VMEM, VMEM, VMEM],
        out_shape=[shape((NB, BLK, DEEP), BF16), sums, sums],
        scratch_shapes=[
            pltpu.SMEM((NB,), jnp.int32),
            pltpu.SMEM((NB,), jnp.int32),
            pltpu.SMEM((CH, W), F32),
            pltpu.VMEM((NB, BLK, BLK), BF16),
            pltpu.VMEM((W, BLK, 2 * BLK), BF16),
            pltpu.VMEM((W, 2, BLK, BLK), BF16),
            scaled,
            pltpu.SemaphoreType.DMA((3,)),
            pltpu.SemaphoreType.DMA((2,)),
            pltpu.SemaphoreType.DMA((2,)),
        ],
        compiler_params=params(12),
        cost_estimate=cost(2 * matmul, 2**23),
        name="product_and_neighbours",
    )(*(in_hbm(x) for x in (left_sector, right_sector, mpo_weight, two_site, left_env, right_env)))
    lower = over_both(to_lower, lambda s, m: (s + 1, m ^ 1 if s % 16 == 15 else m))
    upper = over_both(to_upper, lambda s, m: (s - 1, m ^ 1 if s % 16 == 0 else m))
    own, *slabs = pl.pallas_call(
        second_kernel,
        in_specs=[SMEM, SMEM, VMEM, VMEM],
        out_specs=[VMEM] * (len(Y_HOPS) + 2),
        out_shape=[sums] + [wide_slab] * (len(Y_HOPS) + 1),
        scratch_shapes=[scaled, pltpu.VMEM((NB, BLK, BLK), F32)],
        compiler_params=params(5),
        cost_estimate=cost(matmul, 2**22),
        name="opposite_and_own",
    )(right_sector, mpo_weight, right_env, product)
    opposite = slabs[-1]
    for slab_out, steps in zip(slabs, Y_HOPS):
        opposite = opposite + over_mpo(slab_out, (steps, 0))
    half = N_SEC // 2
    straight = over_both(opposite[0], lambda s, m: (s + half, m))
    crossed = over_both(opposite[1], lambda s, m: (s + half, m ^ 1))
    slabs = pl.pallas_call(
        join_kernel,
        in_specs=[SMEM, SMEM, VMEM, VMEM, VMEM],
        out_specs=[VMEM] * N_MPO,
        out_shape=[slab] * N_MPO,
        cost_estimate=cost(2**21, 2**22),
        compiler_params=params(2),
        name="join_blocks",
    )(src_slot, joining, own, lower, upper)
    moved = [over_mpo(x, hop) for x, hop in zip(slabs, HOPS)]
    return pl.pallas_call(
        last_kernel,
        in_specs=[SMEM, SMEM] + [VMEM] * (N_MPO + 2),
        out_specs=VMEM,
        out_shape=shape((NB, ROWS, BLK), BF16),
        cost_estimate=cost(2**18, 2**20),
        compiler_params=params(2),
        name="sum_and_round",
    )(src_slot, joining, straight, crossed, *moved, slabs[-1])


def solution(mesh):
    placed = (
        P("sec", None, None),
        P("mpo", "sec", None, None),
        P("mpo", "sec", None, None),
        P("sec"),
        P("sec"),
        P("mpo", None),
        P("sec", None),
        P("sec", None),
    )
    return jax.shard_map(
        per_device, mesh=mesh, in_specs=placed, out_specs=P("sec", "mpo", None), check_vma=False
    )
```
